128 devices in a mesh: replica: 16 (over y_lo, z, core), tensor: 8 (over y_hi, x).
Axes of the slice: x: 4, y: 4 (y_hi: 2, y_lo: 2; y = y_hi * 2 + y_lo), z: 4, core: 2. Of those that a mesh axis runs over, the one named last changes fastest.
Arguments:
- hidden: bfloat16 [128, 2, 8192], P('replica'), may hold values from -6 to 6
- shard_rows: float32 [8704, 18432], P(('replica', 'tensor')), may hold values from -0.0625 to 0.0625
- piece_length: int32 [128], replicated, may hold values from 1 to 68, 8192 in all
- cache_keys: bfloat16 [128, 8, 4096, 128], P('replica', 'tensor'), may hold values from -200 to 200
- cache_values: bfloat16 [128, 8, 4096, 128], P('replica', 'tensor'), may hold values from -6 to 6
- cache_fill: int32 [128], P('replica'), may hold values from 1 to 4096, as said below
Outputs:
- layer_out: bfloat16 [128, 2, 8192], P('replica', None, 'tensor')
The draws below stay inside these ranges and needn't reach their ends.
Inputs may be any that keep to these rules, and one draw needn't show every extreme that they name: `piece_length`: the device with replica index r and tensor index t holds piece r times the tensor axis size plus t; some piece has exactly 68 rows. `cache_fill`: some row has a full cache.
All inputs are finite; a program needn't handle non-finite values.
Results may differ from the reference program's by a relative error of at most 0.014.
Values may be sent and summed in bfloat16 or wider, within the bound.
No kernel may reach another device: no remote copies, remote signals or barrier semaphores. Data moves between devices by JAX's collectives and lax.ppermute only.
A program may use at most 192 MiB of HBM per device.

```python
import math
import jax
import jax.numpy as jnp
import numpy as np
from jax import lax

D = 8192
HQ = 64
KV = 8
HD = 128
CL = 4096
BATCH = 128
MAXR = 68
WCOLS = 18432
DEVICES = 128


def draw_cache_fill(key, part):
    first_key, second_key = jax.random.split(key)
    filled = jax.random.randint(first_key, (BATCH,), 1, CL + 1)
    chosen = jax.random.randint(second_key, (), 0, BATCH)
    return jnp.where(jnp.arange(BATCH) == chosen, CL, filled).astype(jnp.int32)


def draw_cache_keys(key, part):
    full_shape = (BATCH, KV, CL, HD)
    return jax.random.normal(key, full_shape, jnp.float32).astype(jnp.bfloat16)


def block_levels(own_key, extent, pieces, least, high):
    def one(dim, shards_of):
        steps = jax.random.uniform(jax.random.fold_in(jax.random.fold_in(own_key, 6), dim), (shards_of,), jnp.float32, least / len(pieces), high / len(pieces))
        return jnp.repeat(jnp.exp(steps), extent[dim] // shards_of).reshape((-1,) + (1,) * (len(extent) - dim - 1))

    level = one(*pieces[0])
    for cut in pieces[1:]:
        level = level * one(*cut)
    return level


def split_up(number_of, total, most, lean):
    weights = [(1 << 20) // math.isqrt(rank ** lean) + 1 for rank in range(2, number_of + 1)]
    spare, given = total - most - (number_of - 1), [1] * (number_of - 1)
    while spare > 0:
        candidates = [i for i in range(number_of - 1) if given[i] < most]
        mass, left = sum([weights[i] for i in candidates]), spare
        for i in candidates:
            more = min(most - given[i], max(1, left * weights[i] // mass), spare)
            given[i] = given[i] + more
            spare = spare - more
    return np.array([most] + given)


def ragged_sizes(stream_key, number_of, total, most, slope):
    if number_of == 2:
        one = jax.random.randint(stream_key, (), max(1, total - most), min(most, total - 1) + 1)
        return jnp.stack([one, total - one])
    tallies = jnp.asarray(split_up(number_of, total, most, slope), jnp.int32)
    twos = (number_of - 1) // 2
    donor, sink = tallies[1:1 + 2 * twos:2], tallies[2:2 + 2 * twos:2]
    slack = jnp.minimum(donor - 1, most - sink)
    shifted = jax.random.randint(jax.random.fold_in(stream_key, 1), (twos,), 0, 1 << 20) % (slack + 1)
    tallies = tallies.at[1:1 + 2 * twos:2].set(donor - shifted).at[2:2 + 2 * twos:2].set(sink + shifted)
    return tallies[jax.random.permutation(jax.random.fold_in(stream_key, 2), number_of)]


def normal_values(stream_key, dims, width, bound, cuts=(), kind=jnp.bfloat16):
    factor_of = block_levels(stream_key, dims, cuts, -0.22, 0.18) if cuts else 1.0
    values = jax.random.normal(stream_key, dims, jnp.float32) * width * factor_of
    return jnp.minimum(jnp.maximum(values, -bound), bound).astype(kind)


def setup_inputs(seed: int = 0) -> dict:
    keys = jax.random.split(jax.random.key(seed), 7)
    return {
        "hidden": normal_values(keys[0], (BATCH, 2, D), 1.0, 6.0, ((0, 16),)),
        "shard_rows": normal_values(keys[1], (DEVICES * MAXR, WCOLS), D ** -0.5, 0.0625, ((0, 128),), jnp.float32),
        "piece_length": ragged_sizes(keys[2], DEVICES, D, MAXR, 1).astype(jnp.int32),
        "cache_keys": draw_cache_keys(jax.random.fold_in(keys[6], 71), 0),
        "cache_values": normal_values(keys[4], (BATCH, KV, CL, HD), 1.0, 6.0, ((0, 16), (1, 8))),
        "cache_fill": draw_cache_fill(jax.random.fold_in(keys[6], 71), 0),
    }


ROPE_BASE = 1000000.0
NEG_FILL = -1e+30

def rotate(source, position):
    halfway = source.shape[-1] // 2
    exponent = jnp.arange(halfway, dtype=jnp.float32) * (2.0 / source.shape[-1])
    frequency = jnp.exp(-exponent * math.log(ROPE_BASE))
    angles = position[:, None, None] * frequency[None, None, :]
    cosine = jnp.cos(angles)
    sine_part = jnp.sin(angles)
    former = source[..., :halfway]
    latter = source[..., halfway:]
    return jnp.concatenate([former * cosine - latter * sine_part, latter * cosine + former * sine_part], axis=-1)

def attend(projected, keys_cache, values_cache, filled):
    batch_rows, heads_kv, span_len, head_size = keys_cache.shape
    count = projected.shape[0]
    width_kv = heads_kv * head_size
    width_q = projected.shape[1] - 2 * width_kv
    heads_q = width_q // head_size
    group_size = heads_q // heads_kv
    position = (filled[:, None] + jnp.arange(2, dtype=jnp.int32)[None, :]).reshape(-1).astype(jnp.float32)
    query = rotate(projected[:, :width_q].reshape(count, heads_q, head_size), position).astype(jnp.bfloat16)
    new_key = rotate(projected[:, width_q:width_q + width_kv].reshape(count, heads_kv, head_size), position).astype(jnp.bfloat16)
    new_value = projected[:, width_q + width_kv:].astype(jnp.bfloat16).reshape(batch_rows, 2, heads_kv, head_size)
    query = query.reshape(batch_rows, 2, heads_kv, group_size, head_size).astype(jnp.float32)
    new_key = new_key.reshape(batch_rows, 2, heads_kv, head_size).astype(jnp.float32)
    factor = 1.0 / math.sqrt(head_size)
    cached = jnp.einsum('bskgd,bkcd->bkgsc', query, keys_cache.astype(jnp.float32)) * factor
    recent = jnp.einsum('bskgd,btkd->bkgst', query, new_key) * factor
    visible = (jnp.arange(span_len)[None, :] < filled[:, None])[:, None, None, None, :]
    causal = jnp.arange(2)[:, None] >= jnp.arange(2)[None, :]
    cached = jnp.where(visible, cached, NEG_FILL)
    recent = jnp.where(causal, recent, NEG_FILL)
    highest = jnp.maximum(lax.optimization_barrier(jnp.max(cached, axis=-1)), lax.optimization_barrier(jnp.max(recent, axis=-1)))
    cached_exp = jnp.exp(cached - highest[..., None])
    recent_exp = jnp.exp(recent - highest[..., None])
    total = lax.optimization_barrier(jnp.sum(cached_exp, axis=-1)) + lax.optimization_barrier(jnp.sum(recent_exp, axis=-1))
    cached_prob = (cached_exp / total[..., None]).astype(jnp.bfloat16).astype(jnp.float32)
    recent_prob = (recent_exp / total[..., None]).astype(jnp.bfloat16).astype(jnp.float32)
    mixed = jnp.einsum('bkgsc,bkcd->bskgd', cached_prob, values_cache.astype(jnp.float32))
    mixed = mixed + jnp.einsum('bkgst,btkd->bskgd', recent_prob, new_value.astype(jnp.float32))
    return mixed.astype(jnp.bfloat16).reshape(count, width_q)

def assemble(shard_rows, piece_length):
    piece_ends = jnp.cumsum(piece_length).astype(jnp.int32)
    starts = (piece_ends - piece_length).astype(jnp.int32)
    global_row = jnp.arange(D, dtype=jnp.int32)
    owners = lax.optimization_barrier(jnp.sum((piece_ends[None, :] <= global_row[:, None]).astype(jnp.int32), axis=1)).astype(jnp.int32)
    within = (global_row - jnp.take(starts, owners)).astype(jnp.int32)
    return jnp.take(shard_rows, (owners * MAXR + within).astype(jnp.int32), axis=0)

def reference(hidden, shard_rows, piece_length, cache_keys, cache_values, cache_fill):
    weights = assemble(shard_rows, piece_length).astype(jnp.bfloat16)
    project_width = (HQ + 2 * KV) * HD
    tokens = hidden.reshape(BATCH * 2, D)
    projected = jnp.dot(tokens, weights[:, :project_width], preferred_element_type=jnp.float32)

    def one_row(items):
        row_proj, row_keys, row_values, row_fill = items
        return attend(row_proj, row_keys[None], row_values[None], row_fill[None])
    attended = lax.map(one_row, (projected.reshape(BATCH, 2, project_width), cache_keys, cache_values, cache_fill))
    attended = attended.reshape(BATCH * 2, HQ * HD)
    output = lax.dot_general(attended, weights[:, project_width:], (((1,), (1,)), ((), ())), preferred_element_type=jnp.float32)
    return output.astype(jnp.bfloat16).reshape(BATCH, 2, D)
```

```python
import math

import jax
import jax.numpy as jnp
from jax import lax
from jax.experimental import pallas as pl
from jax.experimental.pallas import tpu as pltpu
from jax.sharding import PartitionSpec as P

D = 8192
HQ = 64
KV = 8
HD = 128
ROPE_BASE = 1000000.0
NEG_FILL = -1e30
ROWS = 72
WINDOW = 768
LANES = 128


def rope_tables(position):
    halfway = HD // 2
    exponent = jnp.arange(halfway, dtype=jnp.float32) * (2.0 / HD)
    frequency = jnp.exp(-exponent * math.log(ROPE_BASE))
    angles = position[:, None] * frequency[None, :]
    return jnp.cos(angles), jnp.sin(angles)


def rotate(source, cosine, sine_part):
    halfway = source.shape[-1] // 2
    former = source[..., :halfway]
    latter = source[..., halfway:]
    return jnp.concatenate(
        [former * cosine - latter * sine_part, latter * cosine + former * sine_part], axis=-1
    )


def attend(projected, keys_cache, values_cache, filled, cosine, sine_part):
    batch_rows, heads_kv, span_len, head_size = keys_cache.shape
    count = projected.shape[0]
    width_kv = heads_kv * head_size
    width_q = projected.shape[1] - 2 * width_kv
    heads_q = width_q // head_size
    group_size = heads_q // heads_kv
    cosine = cosine[:, None, :]
    sine_part = sine_part[:, None, :]
    query = rotate(
        projected[:, :width_q].reshape(count, heads_q, head_size), cosine, sine_part
    ).astype(jnp.bfloat16)
    new_key = rotate(
        projected[:, width_q : width_q + width_kv].reshape(count, heads_kv, head_size),
        cosine,
        sine_part,
    ).astype(jnp.bfloat16)
    new_value = (
        projected[:, width_q + width_kv :]
        .astype(jnp.bfloat16)
        .reshape(batch_rows, 2, heads_kv, head_size)
    )
    query = query.reshape(batch_rows, 2, heads_kv, group_size, head_size)
    new_key = new_key.reshape(batch_rows, 2, heads_kv, head_size)
    factor = 1.0 / math.sqrt(head_size)
    cached = (
        jnp.einsum("bskgd,bkcd->bkgsc", query, keys_cache, preferred_element_type=jnp.float32)
        * factor
    )
    recent = (
        jnp.einsum("bskgd,btkd->bkgst", query, new_key, preferred_element_type=jnp.float32) * factor
    )
    visible = (jnp.arange(span_len)[None, :] < filled[:, None])[:, None, None, None, :]
    causal = jnp.arange(2)[:, None] >= jnp.arange(2)[None, :]
    cached = jnp.where(visible, cached, NEG_FILL)
    recent = jnp.where(causal, recent, NEG_FILL)
    highest = jnp.maximum(jnp.max(cached, axis=-1), jnp.max(recent, axis=-1))
    cached_exp = jnp.exp(cached - highest[..., None])
    recent_exp = jnp.exp(recent - highest[..., None])
    total = jnp.sum(cached_exp, axis=-1) + jnp.sum(recent_exp, axis=-1)
    cached_prob = (cached_exp / total[..., None]).astype(jnp.bfloat16)
    recent_prob = (recent_exp / total[..., None]).astype(jnp.bfloat16)
    mixed = jnp.einsum(
        "bkgsc,bkcd->bskgd", cached_prob, values_cache, preferred_element_type=jnp.float32
    )
    mixed = mixed + jnp.einsum(
        "bkgst,btkd->bskgd", recent_prob, new_value, preferred_element_type=jnp.float32
    )
    return mixed.astype(jnp.bfloat16).reshape(count, width_q)


def slice_body(q_ref, k_ref, v_ref, o_ref, in_ref, out_ref):
    height = q_ref.shape[0]
    qw, kw = q_ref.shape[1], k_ref.shape[1]
    in_ref[0, 0:height, 0:qw] = q_ref[...].astype(jnp.bfloat16)
    in_ref[0, 0:height, qw : qw + kw] = k_ref[...].astype(jnp.bfloat16)
    in_ref[0, 0:height, qw + kw : qw + 2 * kw] = v_ref[...].astype(jnp.bfloat16)
    in_ref[0, height:ROWS, :] = jnp.zeros((ROWS - height, qw + 2 * kw), jnp.bfloat16)
    out_ref[0, 0:height, :] = o_ref[...].astype(jnp.bfloat16)
    out_ref[0, height:ROWS, :] = jnp.zeros((ROWS - height, qw), jnp.bfloat16)


def split_slices(block, slices):
    height = block.shape[0]
    qw = HQ * HD // slices
    kw = KV * HD // slices
    project = (HQ + 2 * KV) * HD
    return pl.pallas_call(
        slice_body,
        grid=(slices,),
        in_specs=[
            pl.BlockSpec((height, qw), lambda t: (0, t)),
            pl.BlockSpec((height, kw), lambda t: (0, HQ * HD // kw + t)),
            pl.BlockSpec((height, kw), lambda t: (0, (HQ + KV) * HD // kw + t)),
            pl.BlockSpec((height, qw), lambda t: (0, project // qw + t)),
        ],
        out_specs=[
            pl.BlockSpec((1, ROWS, qw + 2 * kw), lambda t: (t, 0, 0)),
            pl.BlockSpec((1, ROWS, qw), lambda t: (t, 0, 0)),
        ],
        out_shape=[
            jax.ShapeDtypeStruct((slices, ROWS, qw + 2 * kw), jnp.bfloat16),
            jax.ShapeDtypeStruct((slices, ROWS, qw), jnp.bfloat16),
        ],
        name="split_slices",
    )(block, block, block, block)


def windows_body(first_ref, tokens_ref, out_ref):
    for index in range(out_ref.shape[0]):
        first = pl.multiple_of(first_ref[index], LANES)
        out_ref[index] = tokens_ref[:, pl.ds(first, WINDOW)]


def token_windows(tokens, first):
    return pl.pallas_call(
        windows_body,
        in_specs=[
            pl.BlockSpec(memory_space=pltpu.SMEM),
            pl.BlockSpec(memory_space=pltpu.VMEM),
        ],
        out_specs=pl.BlockSpec(memory_space=pltpu.VMEM),
        out_shape=jax.ShapeDtypeStruct((first.shape[0], tokens.shape[0], WINDOW), tokens.dtype),
        name="token_windows",
    )(first, tokens)


def place_body(first_ref, part_ref, out_ref, acc_ref):
    acc_ref[...] = jnp.zeros_like(acc_ref)
    for index in range(part_ref.shape[0]):
        first = pl.multiple_of(first_ref[index], LANES)
        acc_ref[:, pl.ds(first, WINDOW)] = acc_ref[:, pl.ds(first, WINDOW)] + part_ref[
            index
        ].astype(jnp.float32)
    width = out_ref.shape[2]
    for index in range(out_ref.shape[0]):
        out_ref[index] = acc_ref[:, index * width : (index + 1) * width].astype(out_ref.dtype)


def place_windows(parts, first, slices):
    count = parts.shape[1]
    return pl.pallas_call(
        place_body,
        in_specs=[
            pl.BlockSpec(memory_space=pltpu.SMEM),
            pl.BlockSpec(memory_space=pltpu.VMEM),
        ],
        out_specs=pl.BlockSpec(memory_space=pltpu.VMEM),
        out_shape=jax.ShapeDtypeStruct((slices, count, D // slices), parts.dtype),
        scratch_shapes=[pltpu.VMEM((count, D), jnp.float32)],
        name="place_windows",
    )(first, parts)


def body(hidden, shard_rows, piece_length, cache_keys, cache_values, cache_fill):
    slices = lax.axis_size("tensor")
    replicas = lax.axis_size("replica")
    replica = lax.axis_index("replica")
    batch_rows = cache_keys.shape[0]
    count = batch_rows * 2
    tokens = hidden.reshape(count, hidden.shape[2])

    piece_ends = jnp.cumsum(piece_length)
    starts = piece_ends - piece_length
    by_replica = starts.reshape(replicas, slices)
    first = jnp.minimum(by_replica[:, 0] // LANES * LANES, D - WINDOW).astype(jnp.int32)
    own_starts = lax.dynamic_index_in_dim(by_replica, replica, 0, keepdims=False)
    own_length = lax.dynamic_index_in_dim(
        piece_length.reshape(replicas, slices), replica, 0, keepdims=False
    )
    own_first = lax.dynamic_index_in_dim(first, replica, 0, keepdims=False)
    offsets = jnp.arange(ROWS, dtype=jnp.int32)
    target = jnp.where(
        offsets[None, :] < own_length[:, None], own_starts[:, None] + offsets[None, :] - own_first, -1
    ).reshape(-1)
    choose = (jnp.arange(WINDOW, dtype=jnp.int32)[:, None] == target[None, :]).astype(jnp.bfloat16)

    project_rows, output_rows = split_slices(shard_rows, slices)
    token_parts = token_windows(tokens, first)
    project_rows = lax.all_to_all(project_rows, "tensor", split_axis=0, concat_axis=0, tiled=True)
    token_parts = lax.all_to_all(token_parts, "replica", split_axis=0, concat_axis=0, tiled=True)
    output_rows = lax.all_to_all(output_rows, "tensor", split_axis=0, concat_axis=0, tiled=True)
    project_rows = project_rows.reshape(slices * ROWS, -1)
    output_rows = output_rows.reshape(slices * ROWS, -1)

    own_tokens = jnp.dot(
        token_parts.reshape(replicas * count, WINDOW), choose, preferred_element_type=jnp.float32
    ).astype(jnp.bfloat16)
    partial = jnp.dot(own_tokens, project_rows, preferred_element_type=jnp.float32)
    partial = partial.astype(jnp.bfloat16).reshape(replicas, count, -1)
    partial = lax.all_to_all(partial, "replica", split_axis=0, concat_axis=0, tiled=True)
    projected = jnp.sum(partial.astype(jnp.float32), axis=0)

    position = (
        (cache_fill[:, None] + jnp.arange(2, dtype=jnp.int32)[None, :])
        .reshape(-1)
        .astype(jnp.float32)
    )
    cosine, sine_part = rope_tables(position)
    attended = attend(projected, cache_keys, cache_values, cache_fill, cosine, sine_part)
    gathered = lax.all_gather(attended, "replica", axis=0, tiled=True)
    output_window = jnp.dot(choose, output_rows, preferred_element_type=jnp.float32).astype(
        jnp.bfloat16
    )
    parts = lax.dot_general(
        gathered, output_window, (((1,), (1,)), ((), ())), preferred_element_type=jnp.float32
    )
    parts = parts.astype(jnp.bfloat16).reshape(replicas, count, WINDOW)
    parts = lax.all_to_all(parts, "replica", split_axis=0, concat_axis=0, tiled=True)
    placed = place_windows(parts, first, slices)
    placed = lax.all_to_all(placed, "tensor", split_axis=0, concat_axis=0, tiled=True)
    result = jnp.sum(placed.astype(jnp.float32), axis=0).astype(jnp.bfloat16)
    return result.reshape(batch_rows, 2, -1)


def solution(mesh):
    placed = (
        P("replica", None, None),
        P(("replica", "tensor"), None),
        P(),
        P("replica", "tensor", None, None),
        P("replica", "tensor", None, None),
        P("replica"),
    )
    return jax.shard_map(
        body, mesh=mesh, in_specs=placed, out_specs=P("replica", None, "tensor"), check_vma=False
    )
```

```python
import math

import jax
import jax.numpy as jnp
from jax import lax
from jax.experimental import pallas as pl
from jax.experimental.pallas import tpu as pltpu
from jax.sharding import PartitionSpec as P

D = 8192
HQ = 64
KV = 8
HD = 128
ROPE_BASE = 1000000.0
NEG_FILL = -1e30
ROWS = 72
WINDOW = 768
LANES = 128


def rope_tables(position):
    halfway = HD // 2
    exponent = jnp.arange(halfway, dtype=jnp.float32) * (2.0 / HD)
    frequency = jnp.exp(-exponent * math.log(ROPE_BASE))
    angles = position[:, None] * frequency[None, :]
    return jnp.cos(angles), jnp.sin(angles)


def rotate(source, cosine, sine_part):
    halfway = source.shape[-1] // 2
    former = source[..., :halfway]
    latter = source[..., halfway:]
    return jnp.concatenate(
        [former * cosine - latter * sine_part, latter * cosine + former * sine_part], axis=-1
    )


def attend(projected, keys_cache, values_cache, filled, cosine, sine_part):
    batch_rows, heads_kv, span_len, head_size = keys_cache.shape
    count = projected.shape[0]
    width_kv = heads_kv * head_size
    width_q = projected.shape[1] - 2 * width_kv
    heads_q = width_q // head_size
    group_size = heads_q // heads_kv
    cosine = cosine[:, None, :]
    sine_part = sine_part[:, None, :]
    query = rotate(
        projected[:, :width_q].reshape(count, heads_q, head_size), cosine, sine_part
    ).astype(jnp.bfloat16)
    new_key = rotate(
        projected[:, width_q : width_q + width_kv].reshape(count, heads_kv, head_size),
        cosine,
        sine_part,
    ).astype(jnp.bfloat16)
    new_value = (
        projected[:, width_q + width_kv :]
        .astype(jnp.bfloat16)
        .reshape(batch_rows, 2, heads_kv, head_size)
    )
    query = query.reshape(batch_rows, 2, heads_kv, group_size, head_size)
    new_key = new_key.reshape(batch_rows, 2, heads_kv, head_size)
    factor = 1.0 / math.sqrt(head_size)
    cached = (
        jnp.einsum("bskgd,bkcd->bkgsc", query, keys_cache, preferred_element_type=jnp.float32)
        * factor
    )
    recent = (
        jnp.einsum("bskgd,btkd->bkgst", query, new_key, preferred_element_type=jnp.float32) * factor
    )
    visible = (jnp.arange(span_len)[None, :] < filled[:, None])[:, None, None, None, :]
    causal = jnp.arange(2)[:, None] >= jnp.arange(2)[None, :]
    cached = jnp.where(visible, cached, NEG_FILL)
    recent = jnp.where(causal, recent, NEG_FILL)
    highest = jnp.maximum(jnp.max(cached, axis=-1), jnp.max(recent, axis=-1))
    cached_exp = jnp.exp(cached - highest[..., None])
    recent_exp = jnp.exp(recent - highest[..., None])
    total = jnp.sum(cached_exp, axis=-1) + jnp.sum(recent_exp, axis=-1)
    cached_prob = (cached_exp / total[..., None]).astype(jnp.bfloat16)
    recent_prob = (recent_exp / total[..., None]).astype(jnp.bfloat16)
    mixed = jnp.einsum(
        "bkgsc,bkcd->bskgd", cached_prob, values_cache, preferred_element_type=jnp.float32
    )
    mixed = mixed + jnp.einsum(
        "bkgst,btkd->bskgd", recent_prob, new_value, preferred_element_type=jnp.float32
    )
    return mixed.astype(jnp.bfloat16).reshape(count, width_q)


def project_body(q_ref, k_ref, v_ref, in_ref):
    height = q_ref.shape[0]
    qw, kw = q_ref.shape[1], k_ref.shape[1]
    in_ref[0, 0:height, 0:qw] = q_ref[...].astype(jnp.bfloat16)
    in_ref[0, 0:height, qw : qw + kw] = k_ref[...].astype(jnp.bfloat16)
    in_ref[0, 0:height, qw + kw : qw + 2 * kw] = v_ref[...].astype(jnp.bfloat16)
    in_ref[0, height:ROWS, :] = jnp.zeros((ROWS - height, qw + 2 * kw), jnp.bfloat16)


def split_project(block, slices):
    height = block.shape[0]
    qw = HQ * HD // slices
    kw = KV * HD // slices
    return pl.pallas_call(
        project_body,
        grid=(slices,),
        in_specs=[
            pl.BlockSpec((height, qw), lambda t: (0, t)),
            pl.BlockSpec((height, kw), lambda t: (0, HQ * HD // kw + t)),
            pl.BlockSpec((height, kw), lambda t: (0, (HQ + KV) * HD // kw + t)),
        ],
        out_specs=pl.BlockSpec((1, ROWS, qw + 2 * kw), lambda t: (t, 0, 0)),
        out_shape=jax.ShapeDtypeStruct((slices, ROWS, qw + 2 * kw), jnp.bfloat16),
        name="split_project",
    )(block, block, block)


def output_body(o_ref, out_ref):
    height, qw = o_ref.shape
    out_ref[0, 0:height, :] = o_ref[...].astype(jnp.bfloat16)
    out_ref[0, height:ROWS, :] = jnp.zeros((ROWS - height, qw), jnp.bfloat16)


def split_output(block, slices):
    height = block.shape[0]
    qw = HQ * HD // slices
    project = (HQ + 2 * KV) * HD
    return pl.pallas_call(
        output_body,
        grid=(slices,),
        in_specs=[pl.BlockSpec((height, qw), lambda t: (0, project // qw + t))],
        out_specs=pl.BlockSpec((1, ROWS, qw), lambda t: (t, 0, 0)),
        out_shape=jax.ShapeDtypeStruct((slices, ROWS, qw), jnp.bfloat16),
        name="split_output",
    )(block)


def windows_body(first_ref, tokens_ref, out_ref):
    for index in range(out_ref.shape[0]):
        first = pl.multiple_of(first_ref[index], LANES)
        out_ref[index] = tokens_ref[:, pl.ds(first, WINDOW)]


def token_windows(tokens, first):
    return pl.pallas_call(
        windows_body,
        in_specs=[
            pl.BlockSpec(memory_space=pltpu.SMEM),
            pl.BlockSpec(memory_space=pltpu.VMEM),
        ],
        out_specs=pl.BlockSpec(memory_space=pltpu.VMEM),
        out_shape=jax.ShapeDtypeStruct((first.shape[0], tokens.shape[0], WINDOW), tokens.dtype),
        name="token_windows",
    )(first, tokens)


def place_body(first_ref, part_ref, out_ref, acc_ref):
    acc_ref[...] = jnp.zeros_like(acc_ref)
    for index in range(part_ref.shape[0]):
        first = pl.multiple_of(first_ref[index], LANES)
        acc_ref[:, pl.ds(first, WINDOW)] = acc_ref[:, pl.ds(first, WINDOW)] + part_ref[
            index
        ].astype(jnp.float32)
    width = out_ref.shape[2]
    for index in range(out_ref.shape[0]):
        out_ref[index] = acc_ref[:, index * width : (index + 1) * width].astype(out_ref.dtype)


def place_windows(parts, first, slices):
    count = parts.shape[1]
    return pl.pallas_call(
        place_body,
        in_specs=[
            pl.BlockSpec(memory_space=pltpu.SMEM),
            pl.BlockSpec(memory_space=pltpu.VMEM),
        ],
        out_specs=pl.BlockSpec(memory_space=pltpu.VMEM),
        out_shape=jax.ShapeDtypeStruct((slices, count, D // slices), parts.dtype),
        scratch_shapes=[pltpu.VMEM((count, D), jnp.float32)],
        name="place_windows",
    )(first, parts)


def exchange_blocks(blocks):
    members = blocks.shape[0]
    mine = lax.axis_index("replica")
    for bit in range(members.bit_length() - 1):
        size = 1 << bit
        low = (mine & size) == 0
        split = blocks.reshape(members // (2 * size), 2, size, *blocks.shape[1:])
        kept = jnp.where(low, split[:, 0], split[:, 1])
        sent = jnp.where(low, split[:, 1], split[:, 0])
        pairs = [(member, member ^ size) for member in range(members)]
        got = lax.ppermute(sent, "replica", pairs)
        blocks = jnp.stack(
            [jnp.where(low, kept, got), jnp.where(low, got, kept)], axis=1
        ).reshape(blocks.shape)
    return blocks


def gather_tokens(block):
    replicas = lax.axis_size("replica")
    count = block.shape[0]
    same_core = [list(range(core, replicas, 2)) for core in range(2)]
    other_core = [(member, member ^ 1) for member in range(replicas)]
    mine = lax.all_gather(block, "replica", axis=0, axis_index_groups=same_core)
    theirs = lax.ppermute(mine, "replica", other_core)
    even = lax.axis_index("replica") % 2 == 0
    pair = [jnp.where(even, mine, theirs), jnp.where(even, theirs, mine)]
    return jnp.stack(pair, axis=1).reshape(replicas * count, -1)


def body(hidden, shard_rows, piece_length, cache_keys, cache_values, cache_fill):
    slices = lax.axis_size("tensor")
    replicas = lax.axis_size("replica")
    replica = lax.axis_index("replica")
    batch_rows = cache_keys.shape[0]
    count = batch_rows * 2

    project_rows, piece_length, hidden = lax.optimization_barrier(
        (split_project(shard_rows, slices), piece_length, hidden)
    )
    project_rows = lax.all_to_all(project_rows, "tensor", split_axis=0, concat_axis=0, tiled=True)
    tokens = hidden.reshape(count, hidden.shape[2])

    piece_ends = jnp.cumsum(piece_length)
    starts = piece_ends - piece_length
    by_replica = starts.reshape(replicas, slices)
    first = jnp.minimum(by_replica[:, 0] // LANES * LANES, D - WINDOW).astype(jnp.int32)
    own_starts = lax.dynamic_index_in_dim(by_replica, replica, 0, keepdims=False)
    own_length = lax.dynamic_index_in_dim(
        piece_length.reshape(replicas, slices), replica, 0, keepdims=False
    )
    own_first = lax.dynamic_index_in_dim(first, replica, 0, keepdims=False)
    offsets = jnp.arange(ROWS, dtype=jnp.int32)
    target = jnp.where(
        offsets[None, :] < own_length[:, None], own_starts[:, None] + offsets[None, :] - own_first, -1
    ).reshape(-1)
    choose = (jnp.arange(WINDOW, dtype=jnp.int32)[:, None] == target[None, :]).astype(jnp.bfloat16)

    token_parts = token_windows(tokens, first)
    token_parts, shard_rows = lax.optimization_barrier((token_parts, shard_rows))
    token_parts = exchange_blocks(token_parts)
    output_rows = split_output(shard_rows, slices)
    output_rows = lax.all_to_all(output_rows, "tensor", split_axis=0, concat_axis=0, tiled=True)
    project_rows = project_rows.reshape(slices * ROWS, -1)
    output_rows = output_rows.reshape(slices * ROWS, -1)

    own_tokens = jnp.dot(
        token_parts.reshape(replicas * count, WINDOW), choose, preferred_element_type=jnp.float32
    ).astype(jnp.bfloat16)
    partial = jnp.dot(own_tokens, project_rows, preferred_element_type=jnp.float32)
    partial = partial.astype(jnp.bfloat16).reshape(replicas, count, -1)
    partial = lax.all_to_all(partial, "replica", split_axis=0, concat_axis=0, tiled=True)
    projected = jnp.sum(partial.astype(jnp.float32), axis=0)

    position = (
        (cache_fill[:, None] + jnp.arange(2, dtype=jnp.int32)[None, :])
        .reshape(-1)
        .astype(jnp.float32)
    )
    cosine, sine_part = rope_tables(position)
    attended = attend(projected, cache_keys, cache_values, cache_fill, cosine, sine_part)
    gathered = gather_tokens(attended)
    output_window = jnp.dot(choose, output_rows, preferred_element_type=jnp.float32).astype(
        jnp.bfloat16
    )
    parts = lax.dot_general(
        gathered, output_window, (((1,), (1,)), ((), ())), preferred_element_type=jnp.float32
    )
    parts = parts.astype(jnp.bfloat16).reshape(replicas, count, WINDOW)
    parts = lax.all_to_all(parts, "replica", split_axis=0, concat_axis=0, tiled=True)
    placed = place_windows(parts, first, slices)
    placed = lax.all_to_all(placed, "tensor", split_axis=0, concat_axis=0, tiled=True)
    result = jnp.sum(placed.astype(jnp.float32), axis=0).astype(jnp.bfloat16)
    return result.reshape(batch_rows, 2, -1)


def solution(mesh):
    placed = (
        P("replica", None, None),
        P(("replica", "tensor"), None),
        P(),
        P("replica", "tensor", None, None),
        P("replica", "tensor", None, None),
        P("replica"),
    )
    return jax.shard_map(
        body, mesh=mesh, in_specs=placed, out_specs=P("replica", None, "tensor"), check_vma=False
    )
```

```python
import math

import jax
import jax.numpy as jnp
from jax import lax
from jax.experimental import pallas as pl
from jax.experimental.pallas import tpu as pltpu
from jax.sharding import PartitionSpec as P

D = 8192
HQ = 64
KV = 8
HD = 128
ROPE_BASE = 1000000.0
NEG_FILL = -1e30
ROWS = 72
WINDOW = 768
LANES = 128


def rope_tables(position):
    halfway = HD // 2
    exponent = jnp.arange(halfway, dtype=jnp.float32) * (2.0 / HD)
    frequency = jnp.exp(-exponent * math.log(ROPE_BASE))
    angles = position[:, None] * frequency[None, :]
    return jnp.cos(angles), jnp.sin(angles)


def rotate(source, cosine, sine_part):
    halfway = source.shape[-1] // 2
    former = source[..., :halfway]
    latter = source[..., halfway:]
    return jnp.concatenate(
        [former * cosine - latter * sine_part, latter * cosine + former * sine_part], axis=-1
    )


def attend(projected, keys_cache, values_cache, filled, cosine, sine_part):
    batch_rows, heads_kv, span_len, head_size = keys_cache.shape
    count = projected.shape[0]
    width_kv = heads_kv * head_size
    width_q = projected.shape[1] - 2 * width_kv
    heads_q = width_q // head_size
    group_size = heads_q // heads_kv
    cosine = cosine[:, None, :]
    sine_part = sine_part[:, None, :]
    query = rotate(
        projected[:, :width_q].reshape(count, heads_q, head_size), cosine, sine_part
    ).astype(jnp.bfloat16)
    new_key = rotate(
        projected[:, width_q : width_q + width_kv].reshape(count, heads_kv, head_size),
        cosine,
        sine_part,
    ).astype(jnp.bfloat16)
    new_value = (
        projected[:, width_q + width_kv :]
        .astype(jnp.bfloat16)
        .reshape(batch_rows, 2, heads_kv, head_size)
    )
    query = query.reshape(batch_rows, 2, heads_kv, group_size, head_size)
    new_key = new_key.reshape(batch_rows, 2, heads_kv, head_size)
    factor = 1.0 / math.sqrt(head_size)
    cached = (
        jnp.einsum("bskgd,bkcd->bkgsc", query, keys_cache, preferred_element_type=jnp.float32)
        * factor
    )
    recent = (
        jnp.einsum("bskgd,btkd->bkgst", query, new_key, preferred_element_type=jnp.float32) * factor
    )
    visible = (jnp.arange(span_len)[None, :] < filled[:, None])[:, None, None, None, :]
    causal = jnp.arange(2)[:, None] >= jnp.arange(2)[None, :]
    cached = jnp.where(visible, cached, NEG_FILL)
    recent = jnp.where(causal, recent, NEG_FILL)
    highest = jnp.maximum(jnp.max(cached, axis=-1), jnp.max(recent, axis=-1))
    cached_exp = jnp.exp(cached - highest[..., None])
    recent_exp = jnp.exp(recent - highest[..., None])
    total = jnp.sum(cached_exp, axis=-1) + jnp.sum(recent_exp, axis=-1)
    cached_prob = (cached_exp / total[..., None]).astype(jnp.bfloat16)
    recent_prob = (recent_exp / total[..., None]).astype(jnp.bfloat16)
    mixed = jnp.einsum(
        "bkgsc,bkcd->bskgd", cached_prob, values_cache, preferred_element_type=jnp.float32
    )
    mixed = mixed + jnp.einsum(
        "bkgst,btkd->bskgd", recent_prob, new_value, preferred_element_type=jnp.float32
    )
    return mixed.astype(jnp.bfloat16).reshape(count, width_q)


def project_body(q_ref, k_ref, v_ref, in_ref):
    height = q_ref.shape[0]
    qw, kw = q_ref.shape[1], k_ref.shape[1]
    in_ref[0, 0:height, 0:qw] = q_ref[...].astype(jnp.bfloat16)
    in_ref[0, 0:height, qw : qw + kw] = k_ref[...].astype(jnp.bfloat16)
    in_ref[0, 0:height, qw + kw : qw + 2 * kw] = v_ref[...].astype(jnp.bfloat16)
    in_ref[0, height:ROWS, :] = jnp.zeros((ROWS - height, qw + 2 * kw), jnp.bfloat16)


def split_project(block, slices):
    height = block.shape[0]
    qw = HQ * HD // slices
    kw = KV * HD // slices
    return pl.pallas_call(
        project_body,
        grid=(slices,),
        in_specs=[
            pl.BlockSpec((height, qw), lambda t: (0, t)),
            pl.BlockSpec((height, kw), lambda t: (0, HQ * HD // kw + t)),
            pl.BlockSpec((height, kw), lambda t: (0, (HQ + KV) * HD // kw + t)),
        ],
        out_specs=pl.BlockSpec((1, ROWS, qw + 2 * kw), lambda t: (t, 0, 0)),
        out_shape=jax.ShapeDtypeStruct((slices, ROWS, qw + 2 * kw), jnp.bfloat16),
        name="split_project",
    )(block, block, block)


def output_body(o_ref, out_ref):
    height, qw = o_ref.shape
    out_ref[0, 0:height, :] = o_ref[...].astype(jnp.bfloat16)
    out_ref[0, height:ROWS, :] = jnp.zeros((ROWS - height, qw), jnp.bfloat16)


def split_output(block, slices):
    height = block.shape[0]
    qw = HQ * HD // slices
    project = (HQ + 2 * KV) * HD
    return pl.pallas_call(
        output_body,
        grid=(slices,),
        in_specs=[pl.BlockSpec((height, qw), lambda t: (0, project // qw + t))],
        out_specs=pl.BlockSpec((1, ROWS, qw), lambda t: (t, 0, 0)),
        out_shape=jax.ShapeDtypeStruct((slices, ROWS, qw), jnp.bfloat16),
        name="split_output",
    )(block)


def windows_body(first_ref, mine_ref, tokens_ref, near_ref, far_ref):
    mine = mine_ref[0]
    for index in range(near_ref.shape[0]):
        near = pl.multiple_of(first_ref[mine ^ (2 * index)], LANES)
        near_ref[index] = tokens_ref[:, pl.ds(near, WINDOW)]
        far = pl.multiple_of(first_ref[mine ^ (2 * index + 1)], LANES)
        far_ref[index] = tokens_ref[:, pl.ds(far, WINDOW)]


def token_windows(tokens, first, mine):
    shape = jax.ShapeDtypeStruct((first.shape[0] // 2, tokens.shape[0], WINDOW), tokens.dtype)
    return pl.pallas_call(
        windows_body,
        in_specs=[
            pl.BlockSpec(memory_space=pltpu.SMEM),
            pl.BlockSpec(memory_space=pltpu.SMEM),
            pl.BlockSpec(memory_space=pltpu.VMEM),
        ],
        out_specs=[pl.BlockSpec(memory_space=pltpu.VMEM)] * 2,
        out_shape=[shape, shape],
        name="token_windows",
    )(first, mine, tokens)


def order_body(mine_ref, *refs):
    mine = mine_ref[0]
    out_ref = refs[-1]
    for index, part_ref in enumerate(refs[:-1]):
        for core in range(2):
            out_ref[mine ^ (2 * index + core)] = part_ref[core]


def order_parts(parts, mine):
    _, count, width = parts[0].shape
    return pl.pallas_call(
        order_body,
        in_specs=[pl.BlockSpec(memory_space=pltpu.SMEM)]
        + [pl.BlockSpec(memory_space=pltpu.VMEM)] * len(parts),
        out_specs=pl.BlockSpec(memory_space=pltpu.VMEM),
        out_shape=jax.ShapeDtypeStruct((2 * len(parts), count, width), parts[0].dtype),
        name="order_parts",
    )(mine, *parts)


def exchange_tokens(near, far, mine):
    members = 2 * near.shape[0]

    def swap(block, step):
        return lax.ppermute(block, "replica", [(m, m ^ step) for m in range(members)])

    both = jnp.stack([near, swap(far, 1)], axis=1)
    parts = [both[0]] + [swap(both[index], 2 * index) for index in range(1, members // 2)]
    return order_parts(parts, mine)


def place_body(first_ref, part_ref, out_ref, acc_ref):
    acc_ref[...] = jnp.zeros_like(acc_ref)
    for index in range(part_ref.shape[0]):
        first = pl.multiple_of(first_ref[index], LANES)
        acc_ref[:, pl.ds(first, WINDOW)] = acc_ref[:, pl.ds(first, WINDOW)] + part_ref[
            index
        ].astype(jnp.float32)
    width = out_ref.shape[2]
    for index in range(out_ref.shape[0]):
        out_ref[index] = acc_ref[:, index * width : (index + 1) * width].astype(out_ref.dtype)


def place_windows(parts, first, slices):
    count = parts.shape[1]
    return pl.pallas_call(
        place_body,
        in_specs=[
            pl.BlockSpec(memory_space=pltpu.SMEM),
            pl.BlockSpec(memory_space=pltpu.VMEM),
        ],
        out_specs=pl.BlockSpec(memory_space=pltpu.VMEM),
        out_shape=jax.ShapeDtypeStruct((slices, count, D // slices), parts.dtype),
        scratch_shapes=[pltpu.VMEM((count, D), jnp.float32)],
        name="place_windows",
    )(first, parts)


def body(hidden, shard_rows, piece_length, cache_keys, cache_values, cache_fill):
    slices = lax.axis_size("tensor")
    replicas = lax.axis_size("replica")
    replica = lax.axis_index("replica")
    batch_rows = cache_keys.shape[0]
    count = batch_rows * 2

    project_rows, piece_length, hidden = lax.optimization_barrier(
        (split_project(shard_rows, slices), piece_length, hidden)
    )
    project_rows = lax.all_to_all(project_rows, "tensor", split_axis=0, concat_axis=0, tiled=True)
    tokens = hidden.reshape(count, hidden.shape[2])

    piece_ends = jnp.cumsum(piece_length)
    starts = piece_ends - piece_length
    by_replica = starts.reshape(replicas, slices)
    first = jnp.minimum(by_replica[:, 0] // LANES * LANES, D - WINDOW).astype(jnp.int32)
    own_starts = lax.dynamic_index_in_dim(by_replica, replica, 0, keepdims=False)
    own_length = lax.dynamic_index_in_dim(
        piece_length.reshape(replicas, slices), replica, 0, keepdims=False
    )
    own_first = lax.dynamic_index_in_dim(first, replica, 0, keepdims=False)
    offsets = jnp.arange(ROWS, dtype=jnp.int32)
    target = jnp.where(
        offsets[None, :] < own_length[:, None], own_starts[:, None] + offsets[None, :] - own_first, -1
    ).reshape(-1)
    choose = (jnp.arange(WINDOW, dtype=jnp.int32)[:, None] == target[None, :]).astype(jnp.bfloat16)

    mine = replica.astype(jnp.int32).reshape(1)
    near, far = token_windows(tokens, first, mine)
    near, shard_rows = lax.optimization_barrier((near, shard_rows))
    token_parts = exchange_tokens(near, far, mine)
    output_rows = split_output(shard_rows, slices)
    output_rows = lax.all_to_all(output_rows, "tensor", split_axis=0, concat_axis=0, tiled=True)
    project_rows = project_rows.reshape(slices * ROWS, -1)
    output_rows = output_rows.reshape(slices * ROWS, -1)

    own_tokens = jnp.dot(
        token_parts.reshape(replicas * count, WINDOW), choose, preferred_element_type=jnp.float32
    ).astype(jnp.bfloat16)
    partial = jnp.dot(own_tokens, project_rows, preferred_element_type=jnp.float32)
    partial = partial.astype(jnp.bfloat16).reshape(replicas, count, -1)
    partial = lax.all_to_all(partial, "replica", split_axis=0, concat_axis=0, tiled=True)
    projected = jnp.sum(partial.astype(jnp.float32), axis=0)

    position = (
        (cache_fill[:, None] + jnp.arange(2, dtype=jnp.int32)[None, :])
        .reshape(-1)
        .astype(jnp.float32)
    )
    cosine, sine_part = rope_tables(position)
    attended = attend(projected, cache_keys, cache_values, cache_fill, cosine, sine_part)
    gathered = lax.all_gather(attended, "replica", axis=0, tiled=True)
    output_window = jnp.dot(choose, output_rows, preferred_element_type=jnp.float32).astype(
        jnp.bfloat16
    )
    parts = lax.dot_general(
        gathered, output_window, (((1,), (1,)), ((), ())), preferred_element_type=jnp.float32
    )
    parts = parts.astype(jnp.bfloat16).reshape(replicas, count, WINDOW)
    parts = lax.all_to_all(parts, "replica", split_axis=0, concat_axis=0, tiled=True)
    placed = place_windows(parts, first, slices)
    placed = lax.all_to_all(placed, "tensor", split_axis=0, concat_axis=0, tiled=True)
    result = jnp.sum(placed.astype(jnp.float32), axis=0).astype(jnp.bfloat16)
    return result.reshape(batch_rows, 2, -1)


def solution(mesh):
    placed = (
        P("replica", None, None),
        P(("replica", "tensor"), None),
        P(),
        P("replica", "tensor", None, None),
        P("replica", "tensor", None, None),
        P("replica"),
    )
    return jax.shard_map(
        body, mesh=mesh, in_specs=placed, out_specs=P("replica", None, "tensor"), check_vma=False
    )
```

```python
import math

import jax
import jax.numpy as jnp
from jax import lax
from jax.experimental import pallas as pl
from jax.experimental.pallas import tpu as pltpu
from jax.sharding import PartitionSpec as P

D = 8192
HQ = 64
KV = 8
HD = 128
ROPE_BASE = 1000000.0
NEG_FILL = -1e30
ROWS = 72
WINDOW = 768
LANES = 128


def rope_tables(position):
    halfway = HD // 2
    exponent = jnp.arange(halfway, dtype=jnp.float32) * (2.0 / HD)
    frequency = jnp.exp(-exponent * math.log(ROPE_BASE))
    angles = position[:, None] * frequency[None, :]
    return jnp.cos(angles), jnp.sin(angles)


def rotate(source, cosine, sine_part):
    halfway = source.shape[-1] // 2
    former = source[..., :halfway]
    latter = source[..., halfway:]
    return jnp.concatenate(
        [former * cosine - latter * sine_part, latter * cosine + former * sine_part], axis=-1
    )


def attend(projected, keys_cache, values_cache, filled, cosine, sine_part):
    batch_rows, heads_kv, span_len, head_size = keys_cache.shape
    count = projected.shape[0]
    width_kv = heads_kv * head_size
    width_q = projected.shape[1] - 2 * width_kv
    heads_q = width_q // head_size
    group_size = heads_q // heads_kv
    cosine = cosine[:, None, :]
    sine_part = sine_part[:, None, :]
    query = rotate(
        projected[:, :width_q].reshape(count, heads_q, head_size), cosine, sine_part
    ).astype(jnp.bfloat16)
    new_key = rotate(
        projected[:, width_q : width_q + width_kv].reshape(count, heads_kv, head_size),
        cosine,
        sine_part,
    ).astype(jnp.bfloat16)
    new_value = (
        projected[:, width_q + width_kv :]
        .astype(jnp.bfloat16)
        .reshape(batch_rows, 2, heads_kv, head_size)
    )
    query = query.reshape(batch_rows, 2, heads_kv, group_size, head_size)
    new_key = new_key.reshape(batch_rows, 2, heads_kv, head_size)
    factor = 1.0 / math.sqrt(head_size)
    cached = (
        jnp.einsum("bskgd,bkcd->bkgsc", query, keys_cache, preferred_element_type=jnp.float32)
        * factor
    )
    recent = (
        jnp.einsum("bskgd,btkd->bkgst", query, new_key, preferred_element_type=jnp.float32) * factor
    )
    visible = (jnp.arange(span_len)[None, :] < filled[:, None])[:, None, None, None, :]
    causal = jnp.arange(2)[:, None] >= jnp.arange(2)[None, :]
    cached = jnp.where(visible, cached, NEG_FILL)
    recent = jnp.where(causal, recent, NEG_FILL)
    highest = jnp.maximum(jnp.max(cached, axis=-1), jnp.max(recent, axis=-1))
    cached_exp = jnp.exp(cached - highest[..., None])
    recent_exp = jnp.exp(recent - highest[..., None])
    total = jnp.sum(cached_exp, axis=-1) + jnp.sum(recent_exp, axis=-1)
    cached_prob = (cached_exp / total[..., None]).astype(jnp.bfloat16)
    recent_prob = (recent_exp / total[..., None]).astype(jnp.bfloat16)
    mixed = jnp.einsum(
        "bkgsc,bkcd->bskgd", cached_prob, values_cache, preferred_element_type=jnp.float32
    )
    mixed = mixed + jnp.einsum(
        "bkgst,btkd->bskgd", recent_prob, new_value, preferred_element_type=jnp.float32
    )
    return mixed.astype(jnp.bfloat16).reshape(count, width_q)


def project_body(q_ref, k_ref, v_ref, in_ref):
    height = q_ref.shape[0]
    qw, kw = q_ref.shape[1], k_ref.shape[1]
    in_ref[0, 0:height, 0:qw] = q_ref[...].astype(jnp.bfloat16)
    in_ref[0, 0:height, qw : qw + kw] = k_ref[...].astype(jnp.bfloat16)
    in_ref[0, 0:height, qw + kw : qw + 2 * kw] = v_ref[...].astype(jnp.bfloat16)
    in_ref[0, height:ROWS, :] = jnp.zeros((ROWS - height, qw + 2 * kw), jnp.bfloat16)


def split_project(block, slices):
    height = block.shape[0]
    qw = HQ * HD // slices
    kw = KV * HD // slices
    return pl.pallas_call(
        project_body,
        grid=(slices,),
        in_specs=[
            pl.BlockSpec((height, qw), lambda t: (0, t)),
            pl.BlockSpec((height, kw), lambda t: (0, HQ * HD // kw + t)),
            pl.BlockSpec((height, kw), lambda t: (0, (HQ + KV) * HD // kw + t)),
        ],
        out_specs=pl.BlockSpec((1, ROWS, qw + 2 * kw), lambda t: (t, 0, 0)),
        out_shape=jax.ShapeDtypeStruct((slices, ROWS, qw + 2 * kw), jnp.bfloat16),
        name="split_project",
    )(block, block, block)


def output_body(o_ref, out_ref):
    height, qw = o_ref.shape
    out_ref[0, 0:height, :] = o_ref[...].astype(jnp.bfloat16)
    out_ref[0, height:ROWS, :] = jnp.zeros((ROWS - height, qw), jnp.bfloat16)


def split_output(block, slices):
    height = block.shape[0]
    qw = HQ * HD // slices
    project = (HQ + 2 * KV) * HD
    return pl.pallas_call(
        output_body,
        grid=(slices,),
        in_specs=[pl.BlockSpec((height, qw), lambda t: (0, project // qw + t))],
        out_specs=pl.BlockSpec((1, ROWS, qw), lambda t: (t, 0, 0)),
        out_shape=jax.ShapeDtypeStruct((slices, ROWS, qw), jnp.bfloat16),
        name="split_output",
    )(block)


def windows_body(first_ref, mine_ref, tokens_ref, near_ref, far_ref):
    mine = mine_ref[0]
    for index in range(near_ref.shape[0]):
        near = pl.multiple_of(first_ref[mine ^ (2 * index)], LANES)
        near_ref[index] = tokens_ref[:, pl.ds(near, WINDOW)]
        far = pl.multiple_of(first_ref[mine ^ (2 * index + 1)], LANES)
        far_ref[index] = tokens_ref[:, pl.ds(far, WINDOW)]


def token_windows(tokens, first, mine):
    shape = jax.ShapeDtypeStruct((first.shape[0] // 2, tokens.shape[0], WINDOW), tokens.dtype)
    return pl.pallas_call(
        windows_body,
        in_specs=[
            pl.BlockSpec(memory_space=pltpu.SMEM),
            pl.BlockSpec(memory_space=pltpu.SMEM),
            pl.BlockSpec(memory_space=pltpu.VMEM),
        ],
        out_specs=[pl.BlockSpec(memory_space=pltpu.VMEM)] * 2,
        out_shape=[shape, shape],
        name="token_windows",
    )(first, mine, tokens)


def order_body(mine_ref, *refs):
    mine = mine_ref[0]
    out_ref = refs[-1]
    for index, part_ref in enumerate(refs[:-1]):
        for core in range(2):
            out_ref[mine ^ (2 * index + core)] = part_ref[core]


def order_parts(parts, mine):
    _, count, width = parts[0].shape
    return pl.pallas_call(
        order_body,
        in_specs=[pl.BlockSpec(memory_space=pltpu.SMEM)]
        + [pl.BlockSpec(memory_space=pltpu.VMEM)] * len(parts),
        out_specs=pl.BlockSpec(memory_space=pltpu.VMEM),
        out_shape=jax.ShapeDtypeStruct((2 * len(parts), count, width), parts[0].dtype),
        name="order_parts",
    )(mine, *parts)


def exchange_tokens(near, far, mine):
    members = 2 * near.shape[0]

    def swap(block, step):
        return lax.ppermute(block, "replica", [(m, m ^ step) for m in range(members)])

    both = jnp.stack([near, swap(far, 1)], axis=1)
    parts = [both[0]] + [swap(both[index], 2 * index) for index in range(1, members // 2)]
    return order_parts(parts, mine)


def place_body(first_ref, mine_ref, part_ref, *refs):
    out_refs, acc_ref = refs[:-1], refs[-1]
    acc_ref[...] = jnp.zeros_like(acc_ref)
    for index in range(part_ref.shape[0]):
        first = pl.multiple_of(first_ref[index], LANES)
        acc_ref[:, pl.ds(first, WINDOW)] = acc_ref[:, pl.ds(first, WINDOW)] + part_ref[
            index
        ].astype(jnp.float32)
    width = out_refs[0].shape[1]
    for index, out_ref in enumerate(out_refs):
        column = pl.multiple_of((mine_ref[0] ^ index) * width, LANES)
        out_ref[...] = acc_ref[:, pl.ds(column, width)].astype(out_ref.dtype)


def place_windows(parts, first, mine, slices):
    count = parts.shape[1]
    return pl.pallas_call(
        place_body,
        in_specs=[
            pl.BlockSpec(memory_space=pltpu.SMEM),
            pl.BlockSpec(memory_space=pltpu.SMEM),
            pl.BlockSpec(memory_space=pltpu.VMEM),
        ],
        out_specs=[pl.BlockSpec(memory_space=pltpu.VMEM)] * slices,
        out_shape=[jax.ShapeDtypeStruct((count, D // slices), parts.dtype)] * slices,
        scratch_shapes=[pltpu.VMEM((count, D), jnp.float32)],
        name="place_windows",
    )(first, mine, parts)


def body(hidden, shard_rows, piece_length, cache_keys, cache_values, cache_fill):
    slices = lax.axis_size("tensor")
    replicas = lax.axis_size("replica")
    replica = lax.axis_index("replica")
    batch_rows = cache_keys.shape[0]
    count = batch_rows * 2

    project_rows, piece_length, hidden = lax.optimization_barrier(
        (split_project(shard_rows, slices), piece_length, hidden)
    )
    project_rows = lax.all_to_all(project_rows, "tensor", split_axis=0, concat_axis=0, tiled=True)
    tokens = hidden.reshape(count, hidden.shape[2])

    piece_ends = jnp.cumsum(piece_length)
    starts = piece_ends - piece_length
    by_replica = starts.reshape(replicas, slices)
    first = jnp.minimum(by_replica[:, 0] // LANES * LANES, D - WINDOW).astype(jnp.int32)
    own_starts = lax.dynamic_index_in_dim(by_replica, replica, 0, keepdims=False)
    own_length = lax.dynamic_index_in_dim(
        piece_length.reshape(replicas, slices), replica, 0, keepdims=False
    )
    own_first = lax.dynamic_index_in_dim(first, replica, 0, keepdims=False)
    offsets = jnp.arange(ROWS, dtype=jnp.int32)
    target = jnp.where(
        offsets[None, :] < own_length[:, None], own_starts[:, None] + offsets[None, :] - own_first, -1
    ).reshape(-1)
    choose = (jnp.arange(WINDOW, dtype=jnp.int32)[:, None] == target[None, :]).astype(jnp.bfloat16)

    mine = replica.astype(jnp.int32).reshape(1)
    near, far = token_windows(tokens, first, mine)
    token_parts = exchange_tokens(near, far, mine)
    project_rows = project_rows.reshape(slices * ROWS, -1)

    own_tokens = jnp.dot(
        token_parts.reshape(replicas * count, WINDOW), choose, preferred_element_type=jnp.float32
    ).astype(jnp.bfloat16)
    partial = jnp.dot(own_tokens, project_rows, preferred_element_type=jnp.float32)
    partial = partial.astype(jnp.bfloat16).reshape(replicas, count, -1)
    partial, shard_rows = lax.optimization_barrier((partial, shard_rows))
    output_rows = split_output(shard_rows, slices)
    partial = lax.all_to_all(partial, "replica", split_axis=0, concat_axis=0, tiled=True)
    output_rows = lax.all_to_all(output_rows, "tensor", split_axis=0, concat_axis=0, tiled=True)
    output_rows = output_rows.reshape(slices * ROWS, -1)
    projected = jnp.sum(partial.astype(jnp.float32), axis=0)

    position = (
        (cache_fill[:, None] + jnp.arange(2, dtype=jnp.int32)[None, :])
        .reshape(-1)
        .astype(jnp.float32)
    )
    cosine, sine_part = rope_tables(position)
    attended = attend(projected, cache_keys, cache_values, cache_fill, cosine, sine_part)
    gathered = lax.all_gather(attended, "replica", axis=0, tiled=True)
    output_window = jnp.dot(choose, output_rows, preferred_element_type=jnp.float32).astype(
        jnp.bfloat16
    )
    parts = lax.dot_general(
        gathered, output_window, (((1,), (1,)), ((), ())), preferred_element_type=jnp.float32
    )
    parts = parts.astype(jnp.bfloat16).reshape(replicas, count, WINDOW)
    parts = lax.all_to_all(parts, "replica", split_axis=0, concat_axis=0, tiled=True)
    own_slice = lax.axis_index("tensor").astype(jnp.int32).reshape(1)
    placed = place_windows(parts, first, own_slice, slices)
    placed = [placed[0]] + [
        lax.ppermute(placed[step], "tensor", [(m, m ^ step) for m in range(slices)])
        for step in range(1, slices)
    ]
    result = sum(block.astype(jnp.float32) for block in placed).astype(jnp.bfloat16)
    return result.reshape(batch_rows, 2, -1)


def solution(mesh):
    placed = (
        P("replica", None, None),
        P(("replica", "tensor"), None),
        P(),
        P("replica", "tensor", None, None),
        P("replica", "tensor", None, None),
        P("replica"),
    )
    return jax.shard_map(
        body, mesh=mesh, in_specs=placed, out_specs=P("replica", None, "tensor"), check_vma=False
    )
```

```python
import math

import jax
import jax.numpy as jnp
from jax import lax
from jax.experimental import pallas as pl
from jax.experimental.pallas import tpu as pltpu
from jax.sharding import PartitionSpec as P

D = 8192
HQ = 64
KV = 8
HD = 128
ROPE_BASE = 1000000.0
NEG_FILL = -1e30
ROWS = 72
WINDOW = 768
LANES = 128


def rope_tables(position):
    halfway = HD // 2
    exponent = jnp.arange(halfway, dtype=jnp.float32) * (2.0 / HD)
    frequency = jnp.exp(-exponent * math.log(ROPE_BASE))
    angles = position[:, None] * frequency[None, :]
    return jnp.cos(angles), jnp.sin(angles)


def rotate(source, cosine, sine_part):
    halfway = source.shape[-1] // 2
    former = source[..., :halfway]
    latter = source[..., halfway:]
    return jnp.concatenate(
        [former * cosine - latter * sine_part, latter * cosine + former * sine_part], axis=-1
    )


def attend(projected, keys_cache, values_cache, filled, cosine, sine_part):
    batch_rows, heads_kv, span_len, head_size = keys_cache.shape
    count = projected.shape[0]
    width_kv = heads_kv * head_size
    width_q = projected.shape[1] - 2 * width_kv
    heads_q = width_q // head_size
    group_size = heads_q // heads_kv
    cosine = cosine[:, None, :]
    sine_part = sine_part[:, None, :]
    query = rotate(
        projected[:, :width_q].reshape(count, heads_q, head_size), cosine, sine_part
    ).astype(jnp.bfloat16)
    new_key = rotate(
        projected[:, width_q : width_q + width_kv].reshape(count, heads_kv, head_size),
        cosine,
        sine_part,
    ).astype(jnp.bfloat16)
    new_value = (
        projected[:, width_q + width_kv :]
        .astype(jnp.bfloat16)
        .reshape(batch_rows, 2, heads_kv, head_size)
    )
    query = query.reshape(batch_rows, 2, heads_kv, group_size, head_size)
    new_key = new_key.reshape(batch_rows, 2, heads_kv, head_size)
    factor = 1.0 / math.sqrt(head_size)
    cached = (
        jnp.einsum("bskgd,bkcd->bkgsc", query, keys_cache, preferred_element_type=jnp.float32)
        * factor
    )
    recent = (
        jnp.einsum("bskgd,btkd->bkgst", query, new_key, preferred_element_type=jnp.float32) * factor
    )
    visible = (jnp.arange(span_len)[None, :] < filled[:, None])[:, None, None, None, :]
    causal = jnp.arange(2)[:, None] >= jnp.arange(2)[None, :]
    cached = jnp.where(visible, cached, NEG_FILL)
    recent = jnp.where(causal, recent, NEG_FILL)
    highest = jnp.maximum(jnp.max(cached, axis=-1), jnp.max(recent, axis=-1))
    cached_exp = jnp.exp(cached - highest[..., None])
    recent_exp = jnp.exp(recent - highest[..., None])
    total = jnp.sum(cached_exp, axis=-1) + jnp.sum(recent_exp, axis=-1)
    cached_prob = (cached_exp / total[..., None]).astype(jnp.bfloat16)
    recent_prob = (recent_exp / total[..., None]).astype(jnp.bfloat16)
    mixed = jnp.einsum(
        "bkgsc,bkcd->bskgd", cached_prob, values_cache, preferred_element_type=jnp.float32
    )
    mixed = mixed + jnp.einsum(
        "bkgst,btkd->bskgd", recent_prob, new_value, preferred_element_type=jnp.float32
    )
    return mixed.astype(jnp.bfloat16).reshape(count, width_q)


def project_body(block_ref, in_ref, q_ref, k_ref, v_ref, sems):
    slices, height, qw = q_ref.shape
    kw = k_ref.shape[2]
    copies = []
    for t in range(slices):
        sources = [
            (t * qw, qw, q_ref),
            (HQ * HD + t * kw, kw, k_ref),
            ((HQ + KV) * HD + t * kw, kw, v_ref),
        ]
        for part, (column, width, target) in enumerate(sources):
            copies.append(
                pltpu.make_async_copy(
                    block_ref.at[:, pl.ds(column, width)], target.at[t], sems.at[t, part]
                )
            )
    for copy in copies:
        copy.start()
    for t in range(slices):
        for copy in copies[3 * t : 3 * t + 3]:
            copy.wait()
        in_ref[t, 0:height, 0:qw] = q_ref[t].astype(jnp.bfloat16)
        in_ref[t, 0:height, qw : qw + kw] = k_ref[t].astype(jnp.bfloat16)
        in_ref[t, 0:height, qw + kw : qw + 2 * kw] = v_ref[t].astype(jnp.bfloat16)
        in_ref[t, height:ROWS, :] = jnp.zeros((ROWS - height, qw + 2 * kw), jnp.bfloat16)


def split_project(block, slices):
    height = block.shape[0]
    qw = HQ * HD // slices
    kw = KV * HD // slices
    return pl.pallas_call(
        project_body,
        in_specs=[pl.BlockSpec(memory_space=pl.ANY)],
        out_specs=pl.BlockSpec(memory_space=pltpu.VMEM),
        out_shape=jax.ShapeDtypeStruct((slices, ROWS, qw + 2 * kw), jnp.bfloat16),
        scratch_shapes=[
            pltpu.VMEM((slices, height, qw), jnp.float32),
            pltpu.VMEM((slices, height, kw), jnp.float32),
            pltpu.VMEM((slices, height, kw), jnp.float32),
            pltpu.SemaphoreType.DMA((slices, 3)),
        ],
        name="split_project",
    )(block)


def output_body(o_ref, out_ref):
    height, qw = o_ref.shape
    out_ref[0, 0:height, :] = o_ref[...].astype(jnp.bfloat16)
    out_ref[0, height:ROWS, :] = jnp.zeros((ROWS - height, qw), jnp.bfloat16)


def split_output(block, slices):
    height = block.shape[0]
    qw = HQ * HD // slices
    project = (HQ + 2 * KV) * HD
    return pl.pallas_call(
        output_body,
        grid=(slices,),
        in_specs=[pl.BlockSpec((height, qw), lambda t: (0, project // qw + t))],
        out_specs=pl.BlockSpec((1, ROWS, qw), lambda t: (t, 0, 0)),
        out_shape=jax.ShapeDtypeStruct((slices, ROWS, qw), jnp.bfloat16),
        name="split_output",
    )(block)


def windows_body(first_ref, mine_ref, tokens_ref, near_ref, far_ref):
    mine = mine_ref[0]
    for index in range(near_ref.shape[0]):
        near = pl.multiple_of(first_ref[mine ^ (2 * index)], LANES)
        near_ref[index] = tokens_ref[:, pl.ds(near, WINDOW)]
        far = pl.multiple_of(first_ref[mine ^ (2 * index + 1)], LANES)
        far_ref[index] = tokens_ref[:, pl.ds(far, WINDOW)]


def token_windows(tokens, first, mine):
    shape = jax.ShapeDtypeStruct((first.shape[0] // 2, tokens.shape[0], WINDOW), tokens.dtype)
    return pl.pallas_call(
        windows_body,
        in_specs=[
            pl.BlockSpec(memory_space=pltpu.SMEM),
            pl.BlockSpec(memory_space=pltpu.SMEM),
            pl.BlockSpec(memory_space=pltpu.VMEM),
        ],
        out_specs=[pl.BlockSpec(memory_space=pltpu.VMEM)] * 2,
        out_shape=[shape, shape],
        name="token_windows",
    )(first, mine, tokens)


def order_body(mine_ref, *refs):
    mine = mine_ref[0]
    out_ref = refs[-1]
    for index, part_ref in enumerate(refs[:-1]):
        for core in range(2):
            out_ref[mine ^ (2 * index + core)] = part_ref[core]


def order_parts(parts, mine):
    _, count, width = parts[0].shape
    return pl.pallas_call(
        order_body,
        in_specs=[pl.BlockSpec(memory_space=pltpu.SMEM)]
        + [pl.BlockSpec(memory_space=pltpu.VMEM)] * len(parts),
        out_specs=pl.BlockSpec(memory_space=pltpu.VMEM),
        out_shape=jax.ShapeDtypeStruct((2 * len(parts), count, width), parts[0].dtype),
        name="order_parts",
    )(mine, *parts)


def exchange_tokens(near, far, mine):
    members = 2 * near.shape[0]

    def swap(block, step):
        return lax.ppermute(block, "replica", [(m, m ^ step) for m in range(members)])

    both = jnp.stack([near, swap(far, 1)], axis=1)
    parts = [both[0]] + [swap(both[index], 2 * index) for index in range(1, members // 2)]
    return order_parts(parts, mine)


def place_body(first_ref, part_ref, out_ref, acc_ref):
    acc_ref[...] = jnp.zeros_like(acc_ref)
    for index in range(part_ref.shape[0]):
        first = pl.multiple_of(first_ref[index], LANES)
        acc_ref[:, pl.ds(first, WINDOW)] = acc_ref[:, pl.ds(first, WINDOW)] + part_ref[
            index
        ].astype(jnp.float32)
    width = out_ref.shape[2]
    for index in range(out_ref.shape[0]):
        out_ref[index] = acc_ref[:, index * width : (index + 1) * width].astype(out_ref.dtype)


def place_windows(parts, first, slices):
    count = parts.shape[1]
    return pl.pallas_call(
        place_body,
        in_specs=[
            pl.BlockSpec(memory_space=pltpu.SMEM),
            pl.BlockSpec(memory_space=pltpu.VMEM),
        ],
        out_specs=pl.BlockSpec(memory_space=pltpu.VMEM),
        out_shape=jax.ShapeDtypeStruct((slices, count, D // slices), parts.dtype),
        scratch_shapes=[pltpu.VMEM((count, D), jnp.float32)],
        name="place_windows",
    )(first, parts)


def body(hidden, shard_rows, piece_length, cache_keys, cache_values, cache_fill):
    slices = lax.axis_size("tensor")
    replicas = lax.axis_size("replica")
    replica = lax.axis_index("replica")
    batch_rows = cache_keys.shape[0]
    count = batch_rows * 2

    project_rows, piece_length, hidden = lax.optimization_barrier(
        (split_project(shard_rows, slices), piece_length, hidden)
    )
    project_rows = lax.all_to_all(project_rows, "tensor", split_axis=0, concat_axis=0, tiled=True)
    tokens = hidden.reshape(count, hidden.shape[2])

    piece_ends = jnp.cumsum(piece_length)
    starts = piece_ends - piece_length
    by_replica = starts.reshape(replicas, slices)
    first = jnp.minimum(by_replica[:, 0] // LANES * LANES, D - WINDOW).astype(jnp.int32)
    own_starts = lax.dynamic_index_in_dim(by_replica, replica, 0, keepdims=False)
    own_length = lax.dynamic_index_in_dim(
        piece_length.reshape(replicas, slices), replica, 0, keepdims=False
    )
    own_first = lax.dynamic_index_in_dim(first, replica, 0, keepdims=False)
    offsets = jnp.arange(ROWS, dtype=jnp.int32)
    target = jnp.where(
        offsets[None, :] < own_length[:, None], own_starts[:, None] + offsets[None, :] - own_first, -1
    ).reshape(-1)
    choose = (jnp.arange(WINDOW, dtype=jnp.int32)[:, None] == target[None, :]).astype(jnp.bfloat16)

    mine = replica.astype(jnp.int32).reshape(1)
    near, far = token_windows(tokens, first, mine)
    near, shard_rows = lax.optimization_barrier((near, shard_rows))
    token_parts = exchange_tokens(near, far, mine)
    output_rows = split_output(shard_rows, slices)
    output_rows = lax.all_to_all(output_rows, "tensor", split_axis=0, concat_axis=0, tiled=True)
    project_rows = project_rows.reshape(slices * ROWS, -1)
    output_rows = output_rows.reshape(slices * ROWS, -1)

    own_tokens = jnp.dot(
        token_parts.reshape(replicas * count, WINDOW), choose, preferred_element_type=jnp.float32
    ).astype(jnp.bfloat16)
    partial = jnp.dot(own_tokens, project_rows, preferred_element_type=jnp.float32)
    partial = partial.astype(jnp.bfloat16).reshape(replicas, count, -1)
    partial = lax.all_to_all(partial, "replica", split_axis=0, concat_axis=0, tiled=True)
    projected = jnp.sum(partial.astype(jnp.float32), axis=0)

    position = (
        (cache_fill[:, None] + jnp.arange(2, dtype=jnp.int32)[None, :])
        .reshape(-1)
        .astype(jnp.float32)
    )
    cosine, sine_part = rope_tables(position)
    attended = attend(projected, cache_keys, cache_values, cache_fill, cosine, sine_part)
    gathered = lax.all_gather(attended, "replica", axis=0, tiled=True)
    output_window = jnp.dot(choose, output_rows, preferred_element_type=jnp.float32).astype(
        jnp.bfloat16
    )
    parts = lax.dot_general(
        gathered, output_window, (((1,), (1,)), ((), ())), preferred_element_type=jnp.float32
    )
    parts = parts.astype(jnp.bfloat16).reshape(replicas, count, WINDOW)
    parts = lax.all_to_all(parts, "replica", split_axis=0, concat_axis=0, tiled=True)
    placed = place_windows(parts, first, slices)
    placed = lax.all_to_all(placed, "tensor", split_axis=0, concat_axis=0, tiled=True)
    result = jnp.sum(placed.astype(jnp.float32), axis=0).astype(jnp.bfloat16)
    return result.reshape(batch_rows, 2, -1)


def solution(mesh):
    placed = (
        P("replica", None, None),
        P(("replica", "tensor"), None),
        P(),
        P("replica", "tensor", None, None),
        P("replica", "tensor", None, None),
        P("replica"),
    )
    return jax.shard_map(
        body, mesh=mesh, in_specs=placed, out_specs=P("replica", None, "tensor"), check_vma=False
    )
```
